32 devices in a mesh: rows: 16 (over z, y, x), cols: 2 (over core).
Axes of the slice: x: 2, y: 2, z: 4, core: 2. Of those that a mesh axis runs over, the one named last changes fastest.
Arguments:
- points: bfloat16 [20480, 512], P('rows', 'cols'), may hold values from -6 to 6
- factor: bfloat16 [20480, 1024], P('rows', 'cols'), may hold values from -2 to 2
- weights: float32 [20480], P('rows'), may hold values from -4 to 4
- pivot_slots: int32 [4, 128], replicated, may hold values from 0 to 1279, as said below
- pivot_owners: int32 [4, 128], replicated, may hold values from 0 to 15
Outputs:
- new_panels: bfloat16 [20480, 512], P('rows', 'cols')
- gram_old: float32 [512, 1024], P('rows', 'cols')
- gram_new: float32 [512, 512], P('rows', 'cols')
The draws below stay inside these ranges and needn't reach their ends.
Inputs may be any that keep to these rules, and one draw needn't show every extreme that they name: Pivot k of panel q is row pivot_slots[q,k] of the block of device pivot_owners[q,k]; the pivots of all panels together are distinct points.
All inputs are finite; a program needn't handle non-finite values.
Results may differ from the reference program's by a relative error of at most 0.009.
Values may be sent and summed in bfloat16 or wider, within the bound.
A program may use at most 64 MiB of HBM per device.

```python
import math
import jax
import jax.numpy as jnp
from jax import lax

F = 512
R = 1024
P_SIZE = 128
PANELS = 4
ROW_DEV = 1280
NPTS = 20480


def pivot_rows_drawn(key):
    order = jax.random.permutation(jax.random.fold_in(key, 29), NPTS)
    picked = order[:PANELS * P_SIZE].astype(jnp.int32).reshape(PANELS, P_SIZE)
    return picked


def draw_pivot_slots(key, part):
    return (pivot_rows_drawn(key) % ROW_DEV).astype(jnp.int32)


def draw_pivot_owners(key, part):
    return (pivot_rows_drawn(key) // ROW_DEV).astype(jnp.int32)


def shard_levels(stream_key, shape, shards, smallest, high):
    loudness, own = 1.0, jax.random.fold_in(stream_key, 6)
    for axis_at, parts in shards:
        draws = jnp.exp(jax.random.uniform(jax.random.fold_in(own, axis_at), (parts,), jnp.float32, smallest / len(shards), high / len(shards)))
        loudness = loudness * jnp.repeat(draws, shape[axis_at] // parts).reshape([-1 if axis == axis_at else 1 for axis in range(len(shape))])
    return loudness


def centred(key, extent, spread, reach, shards=(), held_as=jnp.bfloat16):
    result = spread * jax.random.normal(key, extent, jnp.float32)
    if shards:
        result = result * shard_levels(key, extent, shards, -0.22, 0.18)
    return jnp.clip(result, -reach, reach).astype(held_as)


def setup_inputs(seed: int = 0) -> dict:
    keys = jax.random.split(jax.random.key(seed), 6)
    return {
        "points": centred(keys[0], (NPTS, F), 1.0, 6.0, ((0, 16), (1, 2))),
        "factor": centred(keys[1], (NPTS, R), 0.5, 2.0, ((0, 16), (1, 2))),
        "weights": centred(keys[2], (NPTS,), 1.0, 4.0, ((0, 16),), jnp.float32),
        "pivot_slots": draw_pivot_slots(jax.random.fold_in(keys[5], 71), 0),
        "pivot_owners": draw_pivot_owners(jax.random.fold_in(keys[5], 71), 0),
    }


RIDGE_LEVEL = 1.0

def reference(points, factor, weights, pivot_slots, pivot_owners):
    total = points.shape[0]
    pivot_ids = (pivot_owners * ROW_DEV + pivot_slots).astype(jnp.int32)
    norms = lax.optimization_barrier(jnp.sum(jnp.square(points.astype(jnp.float32)), axis=1))
    built = jnp.zeros((total, PANELS * P_SIZE), jnp.bfloat16)
    row_ids = jnp.arange(total, dtype=jnp.int32)
    identity = jnp.eye(P_SIZE, dtype=jnp.float32)
    for index in range(PANELS):
        chosen = pivot_ids[index]
        sel_points = points[chosen]
        sel_factor = factor[chosen]
        sel_built = built[chosen]
        sel_norms = norms[chosen]
        cross = jnp.dot(points.astype(jnp.float32), sel_points.T.astype(jnp.float32), preferred_element_type=jnp.float32)
        dist = norms[:, None] + sel_norms[None, :] - 2.0 * cross
        schur = jnp.dot(factor.astype(jnp.float32), sel_factor.T.astype(jnp.float32), preferred_element_type=jnp.float32)
        ridge = jnp.where(row_ids[:, None] == chosen[None, :], RIDGE_LEVEL, 0.0).astype(jnp.float32)
        columns = jnp.exp(-dist / F) + ridge + schur / (3.0 * R) - jnp.dot(built.astype(jnp.float32), sel_built.T.astype(jnp.float32), preferred_element_type=jnp.float32)
        block_dist = sel_norms[:, None] + sel_norms[None, :] - 2.0 * jnp.dot(sel_points.astype(jnp.float32), sel_points.T.astype(jnp.float32), preferred_element_type=jnp.float32)
        block = jnp.exp(-block_dist / F) + RIDGE_LEVEL * identity + jnp.dot(sel_factor.astype(jnp.float32), sel_factor.T.astype(jnp.float32), preferred_element_type=jnp.float32) / (3.0 * R) - jnp.dot(sel_built.astype(jnp.float32), sel_built.T.astype(jnp.float32), preferred_element_type=jnp.float32)
        lower = jnp.linalg.cholesky(block)
        inverse = lax.linalg.triangular_solve(lower, identity, left_side=True, lower=True)
        fresh = jnp.dot(columns, inverse.T, precision=lax.Precision.HIGHEST).astype(jnp.bfloat16)
        built = built.at[:, index * P_SIZE:(index + 1) * P_SIZE].set(fresh)
    weighted = (built.astype(jnp.float32) * weights[:, None]).astype(jnp.bfloat16)
    dims = (((0,), (0,)), ((), ()))
    scale = P_SIZE / math.sqrt(total)
    gram_old = lax.dot_general(weighted.astype(jnp.float32), factor.astype(jnp.float32), dims, preferred_element_type=jnp.float32) * scale
    gram_new = lax.dot_general(weighted.astype(jnp.float32), built.astype(jnp.float32), dims, preferred_element_type=jnp.float32) * scale
    return (built, gram_old, gram_new)
```

```python
import functools
import math

import jax
import jax.numpy as jnp
from jax import lax
from jax.experimental import pallas as pl
from jax.experimental.pallas import tpu as pltpu
from jax.sharding import PartitionSpec as P

RIDGE_LEVEL = 1.0
BLOCK = 8
VMEM = pltpu.VMEM
HIGH = lax.Precision.HIGHEST
NT = (((1,), (1,)), ((), ()))
TN = (((0,), (0,)), ((), ()))


def inner_size(rows):
    inner = 1
    while inner * inner * 4 <= rows:
        inner *= 2
    return inner


def remote(src, dst, send, recv, row, col):
    return pltpu.make_async_remote_copy(
        src_ref=src, dst_ref=dst, send_sem=send, recv_sem=recv,
        device_id=(row, col), device_id_type=pl.DeviceIdType.MESH,
    )


def greet(me, col, inner, outer):
    place, layer = me % inner, me // inner
    barrier = pltpu.get_barrier_semaphore()
    peers = [(me, 1 - col)]
    peers += [(layer * inner + (place + d) % inner, col) for d in range(1, inner)]
    peers += [(((layer + d) % outer) * inner + place, col) for d in range(1, outer)]
    for peer in peers:
        pl.semaphore_signal(barrier, inc=1, device_id=peer, device_id_type=pl.DeviceIdType.MESH)
    pl.semaphore_wait(barrier, len(peers))


def pick_kernel(ids_ref, points_ref, factor_ref, out_ref):
    here = points_ref.shape[0]
    first = lax.axis_index("rows") * here
    ids = ids_ref[...]
    spots = lax.broadcasted_iota(jnp.int32, (ids.shape[0], here), 1) + first
    hot = jnp.where(spots == ids, 1.0, 0.0).astype(jnp.bfloat16)
    width = points_ref.shape[1]
    out_ref[:, :width] = jnp.dot(hot, points_ref[...], preferred_element_type=jnp.float32).astype(jnp.bfloat16)
    out_ref[:, width:] = jnp.dot(hot, factor_ref[...], preferred_element_type=jnp.float32).astype(jnp.bfloat16)


def pivot_kernel(inner, outer, part, points, factor, piv, other_points, other_factor,
                 buf_a, buf_b, acc, a_send, a_recv, b_send, b_recv, c_send, c_recv,
                 d_send, d_recv, e_send, e_recv, x_send, x_recv):
    me = lax.axis_index("rows")
    col = lax.axis_index("cols")
    place, layer = me % inner, me // inner
    half = other_points.shape[0]
    greet(me, col, inner, outer)
    sent = []
    stage = []
    for d in range(1, inner):
        p = (place + d) % inner
        c = remote(part.at[:, p], buf_a.at[d - 1], a_send.at[d - 1], a_recv.at[d - 1], layer * inner + p, col)
        c.start()
        stage.append(c)
    theirs = pl.ds(pl.multiple_of((1 - col) * half, 16), half)
    swap = [
        remote(points.at[theirs], other_points, x_send.at[0], x_recv.at[0], me, 1 - col),
        remote(factor.at[theirs], other_factor, x_send.at[1], x_recv.at[1], me, 1 - col),
    ]
    for c in swap:
        c.start()
    total = part[:, place]
    for c in stage:
        c.wait_recv()
    for d in range(1, inner):
        total = total + buf_a[d - 1]
    acc[...] = total
    sent += stage
    stage = []
    for d in range(1, outer):
        z = (layer + d) % outer
        c = remote(acc.at[z], buf_b.at[d - 1], b_send.at[d - 1], b_recv.at[d - 1], z * inner + place, col)
        c.start()
        stage.append(c)
    mine = acc[layer]
    for c in stage:
        c.wait_recv()
    for d in range(1, outer):
        mine = mine + buf_b[d - 1]
    piv[col, layer, place] = mine
    sent += stage
    stage = []
    for d in range(1, outer):
        z = (layer + d) % outer
        c = remote(piv.at[col, layer, place], piv.at[col, layer, place], c_send.at[d - 1], c_recv.at[d - 1],
                   z * inner + place, col)
        c.start()
        stage.append(c)
    for c in stage:
        c.wait_recv()
    sent += stage
    stage = []
    for d in range(1, inner):
        p = (place + d) % inner
        c = remote(piv.at[col, :, place], piv.at[col, :, place], d_send.at[d - 1], d_recv.at[d - 1],
                   layer * inner + p, col)
        c.start()
        stage.append(c)
    last = []
    for d in range(inner):
        p = (place + inner - d) % inner
        if d:
            stage[d - 1].wait_recv()
        c = remote(piv.at[col, :, p], piv.at[col, :, p], e_send.at[d], e_recv.at[d], me, 1 - col)
        c.start()
        last.append(c)
    sent += stage
    for c in last + swap:
        c.wait_recv()
    for c in sent + last + swap:
        c.wait_send()


def factor_block(size, a, e, rows, outs, wide):
    for first in range(0, size, BLOCK):
        span = slice(first, first + BLOCK)
        strip = a[span, :]
        for k in range(BLOCK):
            wide[k] = jnp.broadcast_to(strip[:, first + k:first + k + 1], (BLOCK, size))
        d = {(i, k): wide[k, i:i + 1, :] for i in range(BLOCK) for k in range(i + 1)}
        r = [a[first + i:first + i + 1, :] for i in range(BLOCK)]
        s = [e[first + i:first + i + 1, :] for i in range(BLOCK)]
        for k in range(BLOCK):
            scale = lax.rsqrt(d[k, k])
            r[k] = r[k] * scale
            s[k] = s[k] * scale
            for i in range(k + 1, BLOCK):
                d[i, k] = d[i, k] * scale
            for i in range(k + 1, BLOCK):
                r[i] = r[i] - d[i, k] * r[k]
                s[i] = s[i] - d[i, k] * s[k]
                for m in range(k + 1, i + 1):
                    d[i, m] = d[i, m] - d[i, k] * d[m, k]
        for k in range(BLOCK):
            rows[k:k + 1, :] = r[k]
            e[first + k:first + k + 1, :] = s[k]
        after = first + BLOCK
        if after < size:
            upper = jnp.transpose(rows[...])
            rest_a = a[after:, :]
            rest_e = e[after:, :]
            for k in range(BLOCK):
                column = upper[after:, k:k + 1]
                rest_a = rest_a - column * rows[k:k + 1, :]
                rest_e = rest_e - column * e[first + k:first + k + 1, :]
            a[after:, :] = rest_a
            e[after:, :] = rest_e


def panel_kernel(panels, ids_ref, piv, points, factor, other_points, other_factor, out_ref,
                 cols, pan, a, e, rows, wide):
    me = lax.axis_index("rows")
    col = lax.axis_index("cols")
    here, fw = points.shape
    half = here // 2
    size = cols.shape[2]
    feats, rank = 2 * fw, 2 * factor.shape[1]
    mine = pl.ds(pl.multiple_of(col * half, 16), half)
    p_self, p_other = piv.at[col], piv.at[1 - col]
    f32 = jnp.float32

    def norm(x, y):
        x, y = x.astype(f32), y.astype(f32)
        return jnp.sum(x * x, axis=1, keepdims=True) + jnp.sum(y * y, axis=1, keepdims=True)

    own_norm = norm(points[mine, :], other_points[...])
    piv_norm = norm(p_self[:, :fw], p_other[:, :fw])
    first = me * here + col * half
    own_ids = lax.broadcasted_iota(jnp.int32, (half, size), 0) + first
    place_r = lax.broadcasted_iota(jnp.int32, (panels * size, size), 0)
    place_c = lax.broadcasted_iota(jnp.int32, (panels * size, size), 1)

    def dot(x, y):
        return lax.dot_general(x, y, NT, preferred_element_type=f32)

    for q in range(panels):
        span = slice(q * size, (q + 1) * size)
        ps, po = p_self[span, :], p_other[span, :]
        row_norm = jnp.transpose(jnp.broadcast_to(piv_norm[span, :], (size, size)))[0:1, :]

        def entries(xs, xo, ys, yo, n, same):
            cross = dot(xs, ps[:, :fw]) + dot(xo, po[:, :fw])
            schur = dot(ys, ps[:, fw:]) + dot(yo, po[:, fw:])
            dist = n + row_norm - 2.0 * cross
            return jnp.exp(-dist / feats) + jnp.where(same, RIDGE_LEVEL, 0.0) + schur / (3.0 * rank)

        cols[q, :half, :] = entries(points[mine, :], other_points[...], factor[mine, :], other_factor[...],
                                    own_norm, own_ids == ids_ref[:, span])
        cols[q, half:, :] = entries(p_self[:, :fw], p_other[:, :fw], p_self[:, fw:], p_other[:, fw:],
                                    piv_norm, place_r == place_c + q * size)
    eye = jnp.where(place_r[:size, :] == place_c[:size, :], 1.0, 0.0)

    @pl.loop(0, panels)
    def _(q):
        e[...] = eye
        a[...] = cols[q, pl.ds(pl.multiple_of(half + q * size, 8), size), :]
        factor_block(size, a, e, rows, None, wide)
        pan[...] = lax.dot_general(cols[q], e[...], NT, precision=HIGH,
                                   preferred_element_type=f32).astype(jnp.bfloat16)
        out_ref[:, pl.ds(pl.multiple_of(q * size, size), size)] = pan[:half, :]
        for later in range(1, panels):
            @pl.when(later > q)
            def _():
                cols[later] = cols[later] - dot(pan[...], pan[half + later * size:half + (later + 1) * size, :])


def gram_kernel(inner, outer, scale, built, factor, weights, own_cols, gram,
                theirs, part, keep, buf_a, mid, acc, buf_b,
                a_send, a_recv, b_send, b_recv, x_send, x_recv):
    me = lax.axis_index("rows")
    col = lax.axis_index("cols")
    place, layer = me % inner, me // inner
    half, wide = built.shape
    width = own_cols.shape[1]
    rank = factor.shape[1]
    chunk = gram.shape[0]
    f32 = jnp.float32
    greet(me, col, inner, outer)
    swap = remote(built, theirs, x_send, x_recv, me, 1 - col)
    swap.start()
    lanes = pl.ds(pl.multiple_of(col * width, 128), width)

    def add(source, which, start):
        span = pl.ds(pl.multiple_of(which * half, 16), half)
        weighted = (source[...].astype(f32) * weights[span, :]).astype(jnp.bfloat16)
        own = source[:, lanes]
        own_cols[span, :] = own
        old = lax.dot_general(weighted, factor[span, :], TN, preferred_element_type=f32)
        new = lax.dot_general(weighted, own, TN, preferred_element_type=f32)
        if start:
            keep[:, :rank] = old
            keep[:, rank:] = new
        else:
            keep[:, :rank] = (keep[:, :rank] + old) * scale
            keep[:, rank:] = (keep[:, rank:] + new) * scale

    add(built, col, True)
    swap.wait_recv()
    add(theirs, 1 - col, False)
    for z in range(outer):
        for p in range(inner):
            first = (z * inner + p) * chunk
            part[z, p] = keep[first:first + chunk, :].astype(jnp.bfloat16)
    stage = []
    for d in range(1, inner):
        p = (place + d) % inner
        c = remote(part.at[:, p], buf_a.at[d - 1], a_send.at[d - 1], a_recv.at[d - 1], layer * inner + p, col)
        c.start()
        stage.append(c)
    for z in range(outer):
        acc[z] = keep[pl.ds(pl.multiple_of((z * inner + place) * chunk, 8), chunk), :]
    for d in range(1, inner):
        stage[d - 1].wait_recv()
        acc[...] = acc[...] + buf_a[d - 1].astype(f32)
    mid[...] = acc[...].astype(jnp.bfloat16)
    second = []
    for d in range(1, outer):
        z = (layer + d) % outer
        c = remote(mid.at[z], buf_b.at[d - 1], b_send.at[d - 1], b_recv.at[d - 1], z * inner + place, col)
        c.start()
        second.append(c)
    total = acc[layer]
    for d in range(1, outer):
        second[d - 1].wait_recv()
        total = total + buf_b[d - 1].astype(f32)
    gram[...] = total
    for c in stage + second + [swap]:
        c.wait_send()


def body(points, factor, weights, pivot_slots, pivot_owners):
    here, fw = points.shape
    rank = factor.shape[1]
    panels, size = pivot_slots.shape
    rows = lax.axis_size("rows")
    inner = inner_size(rows)
    outer = rows // inner
    count = panels * size
    chunk = count // rows
    width = fw + rank
    half = here // 2
    bf16, f32 = jnp.bfloat16, jnp.float32
    ids = (pivot_owners * here + pivot_slots).reshape(count)
    vm = pl.BlockSpec(memory_space=VMEM)
    sem = lambda n: pltpu.SemaphoreType.DMA((n,))
    limit = 60 * 1024 * 1024

    part = pl.pallas_call(
        pick_kernel,
        out_shape=jax.ShapeDtypeStruct((count, width), bf16),
        in_specs=[vm] * 3, out_specs=vm, name="pick",
        compiler_params=pltpu.CompilerParams(vmem_limit_bytes=limit),
    )(ids[:, None], points, factor)

    piv, other_points, other_factor = pl.pallas_call(
        functools.partial(pivot_kernel, inner, outer),
        out_shape=(
            jax.ShapeDtypeStruct((2, outer, inner, chunk, width), bf16),
            jax.ShapeDtypeStruct((half, fw), bf16),
            jax.ShapeDtypeStruct((half, rank), bf16),
        ),
        in_specs=[vm] * 3, out_specs=(vm,) * 3, name="pivots",
        scratch_shapes=[
            VMEM((inner - 1, outer, chunk, width), bf16),
            VMEM((outer - 1, chunk, width), bf16),
            VMEM((outer, chunk, width), bf16),
            sem(inner - 1), sem(inner - 1), sem(outer - 1), sem(outer - 1),
            sem(outer - 1), sem(outer - 1), sem(inner - 1), sem(inner - 1),
            sem(inner), sem(inner), sem(2), sem(2),
        ],
        compiler_params=pltpu.CompilerParams(collective_id=0, has_side_effects=True, vmem_limit_bytes=limit),
    )(part.reshape(outer, inner, chunk, width), points, factor)

    built = pl.pallas_call(
        functools.partial(panel_kernel, panels),
        out_shape=jax.ShapeDtypeStruct((half, count), bf16),
        in_specs=[vm] * 6, out_specs=vm, name="panels",
        scratch_shapes=[
            VMEM((panels, half + count, size), f32),
            VMEM((half + count, size), bf16),
            VMEM((size, size), f32), VMEM((size, size), f32),
            VMEM((BLOCK, size), f32), VMEM((BLOCK, BLOCK, size), f32),
        ],
        compiler_params=pltpu.CompilerParams(vmem_limit_bytes=limit),
    )(ids[None, :], piv.reshape(2, count, width), points, factor, other_points, other_factor)

    scale = size / math.sqrt(here * rows)
    gw = rank + count // 2
    own_cols, gram = pl.pallas_call(
        functools.partial(gram_kernel, inner, outer, scale),
        out_shape=(
            jax.ShapeDtypeStruct((here, count // 2), bf16),
            jax.ShapeDtypeStruct((chunk, gw), f32),
        ),
        in_specs=[vm] * 3, out_specs=(vm,) * 2, name="gram",
        scratch_shapes=[
            VMEM((half, count), bf16),
            VMEM((outer, inner, chunk, gw), bf16),
            VMEM((count, gw), f32),
            VMEM((inner - 1, outer, chunk, gw), bf16),
            VMEM((outer, chunk, gw), bf16),
            VMEM((outer, chunk, gw), f32),
            VMEM((outer - 1, chunk, gw), bf16),
            sem(inner - 1), sem(inner - 1), sem(outer - 1), sem(outer - 1),
            pltpu.SemaphoreType.DMA, pltpu.SemaphoreType.DMA,
        ],
        compiler_params=pltpu.CompilerParams(collective_id=1, has_side_effects=True, vmem_limit_bytes=limit),
    )(built, factor, weights[:, None])
    return own_cols, gram[:, :rank], gram[:, rank:]


def solution(mesh):
    return jax.shard_map(
        body,
        mesh=mesh,
        in_specs=(P("rows", "cols"), P("rows", "cols"), P("rows"), P(), P()),
        out_specs=(P("rows", "cols"), P("rows", "cols"), P("rows", "cols")),
        check_vma=False,
    )
```

```python
import functools
import math

import jax
import jax.numpy as jnp
from jax import lax
from jax.experimental import pallas as pl
from jax.experimental.pallas import tpu as pltpu
from jax.sharding import PartitionSpec as P

RIDGE_LEVEL = 1.0
BLOCK = 8
VMEM = pltpu.VMEM
HIGH = lax.Precision.HIGHEST
NT = (((1,), (1,)), ((), ()))
TN = (((0,), (0,)), ((), ()))


def inner_size(rows):
    inner = 1
    while inner * inner * 4 <= rows:
        inner *= 2
    return inner


def remote(src, dst, send, recv, row, col):
    return pltpu.make_async_remote_copy(
        src_ref=src, dst_ref=dst, send_sem=send, recv_sem=recv,
        device_id=(row, col), device_id_type=pl.DeviceIdType.MESH,
    )


def greet(me, col, inner, outer):
    place, layer = me % inner, me // inner
    barrier = pltpu.get_barrier_semaphore()
    peers = [(me, 1 - col)]
    peers += [(layer * inner + (place + d) % inner, col) for d in range(1, inner)]
    peers += [(((layer + d) % outer) * inner + place, col) for d in range(1, outer)]
    for peer in peers:
        pl.semaphore_signal(barrier, inc=1, device_id=peer, device_id_type=pl.DeviceIdType.MESH)
    pl.semaphore_wait(barrier, len(peers))


def factor_block(size, a, e, rows, outs, wide):
    for first in range(0, size, BLOCK):
        span = slice(first, first + BLOCK)
        strip = a[span, :]
        for k in range(BLOCK):
            wide[k] = jnp.broadcast_to(strip[:, first + k:first + k + 1], (BLOCK, size))
        d = {(i, k): wide[k, i:i + 1, :] for i in range(BLOCK) for k in range(i + 1)}
        r = [a[first + i:first + i + 1, :] for i in range(BLOCK)]
        s = [e[first + i:first + i + 1, :] for i in range(BLOCK)]
        for k in range(BLOCK):
            scale = lax.rsqrt(d[k, k])
            r[k] = r[k] * scale
            s[k] = s[k] * scale
            for i in range(k + 1, BLOCK):
                d[i, k] = d[i, k] * scale
            for i in range(k + 1, BLOCK):
                r[i] = r[i] - d[i, k] * r[k]
                s[i] = s[i] - d[i, k] * s[k]
                for m in range(k + 1, i + 1):
                    d[i, m] = d[i, m] - d[i, k] * d[m, k]
        for k in range(BLOCK):
            rows[k:k + 1, :] = r[k]
            e[first + k:first + k + 1, :] = s[k]
        after = first + BLOCK
        if after < size:
            upper = jnp.transpose(rows[...])
            rest_a = a[after:, :]
            rest_e = e[after:, :]
            for k in range(BLOCK):
                column = upper[after:, k:k + 1]
                rest_a = rest_a - column * rows[k:k + 1, :]
                rest_e = rest_e - column * e[first + k:first + k + 1, :]
            a[after:, :] = rest_a
            e[after:, :] = rest_e


def panel_kernel(inner, outer, slots, owners, points, factor, out_ref,
                 part, piv, other_points, other_factor, buf_a, buf_b, acc,
                 prow, inv, norms, a, rows, wide,
                 a_send, a_recv, b_send, b_recv, c_send, c_recv,
                 d_send, d_recv, e_send, e_recv, x_send, x_recv):
    me = lax.axis_index("rows")
    col = lax.axis_index("cols")
    place, layer = me % inner, me // inner
    panels, size = slots.shape
    here, fw = points.shape
    half = here // 2
    feats, rank = 2 * fw, 2 * factor.shape[1]
    chunk = size // inner
    f32, bf16 = jnp.float32, jnp.bfloat16
    greet(me, col, inner, outer)

    def piece(q, p):
        return pl.ds(pl.multiple_of(q * size + p * chunk, chunk), chunk)

    def turned(row):
        return jnp.transpose(jnp.broadcast_to(row, (size, size)))

    spots = lax.broadcasted_iota(jnp.int32, (size, here), 1) + me * here
    step_a = []
    for q in range(panels):
        ids = (owners[q:q + 1, :] * here + slots[q:q + 1, :]).astype(f32)
        hot = jnp.where(spots == turned(ids)[:, 0:1].astype(jnp.int32), 1.0, 0.0).astype(bf16)
        span = slice(q * size, (q + 1) * size)
        part[span, :fw] = jnp.dot(hot, points[...], preferred_element_type=f32).astype(bf16)
        part[span, fw:] = jnp.dot(hot, factor[...], preferred_element_type=f32).astype(bf16)
        for d in range(1, inner):
            p = (place + d) % inner
            c = remote(part.at[piece(q, p)], buf_a.at[q, d - 1], a_send.at[q, d - 1], a_recv.at[q, d - 1],
                       layer * inner + p, col)
            c.start()
            step_a.append(c)
    theirs = pl.ds(pl.multiple_of((1 - col) * half, 16), half)
    swap = [
        remote(points.at[theirs], other_points, x_send.at[0], x_recv.at[0], me, 1 - col),
        remote(factor.at[theirs], other_factor, x_send.at[1], x_recv.at[1], me, 1 - col),
    ]
    for c in swap:
        c.start()

    def to_owner(q):
        return remote(acc.at[q], buf_b.at[layer], b_send.at[q], b_recv.at[layer], q * inner + place, col)

    def from_layer(z):
        return remote(acc.at[0], buf_b.at[z], b_send.at[0], b_recv.at[z], z * inner + place, col)

    def spread(q, z):
        here_it = piv.at[col, piece(q, place)]
        return remote(here_it, here_it, c_send.at[z], c_recv.at[q], z * inner + place, col)

    def around(q, d):
        it = piv.at[col, piece(q, place)]
        return remote(it, it, d_send.at[q, d - 1], d_recv.at[q, d - 1], layer * inner + (place + d) % inner, col)

    def across(q, d):
        it = piv.at[col, piece(q, (place + inner - d) % inner)]
        return remote(it, it, e_send.at[q, d], e_recv.at[q, d], me, 1 - col)

    def collect(q):
        @pl.when(layer == q)
        def _():
            mine = acc[q]
            for d in range(1, outer):
                z = (q + d) % outer
                from_layer(z).wait_recv()
                mine = mine + buf_b[z]
            piv[col, piece(q, place)] = mine
            for d in range(1, outer):
                spread(q, (q + d) % outer).start()

    for q in range(panels):
        total = part[piece(q, place), :]
        for d in range(1, inner):
            step_a[q * (inner - 1) + d - 1].wait_recv()
            total = total + buf_a[q, d - 1]
        acc[q] = total

        @pl.when(layer != q)
        def _():
            to_owner(q).start()
        if q:
            collect(q - 1)
    collect(panels - 1)
    for q in range(panels):
        @pl.when(layer != q)
        def _():
            spread(q, layer).wait_recv()
        for d in range(1, inner):
            around(q, d).start()
        across(q, 0).start()

    def forward(q):
        for d in range(1, inner):
            around(q, d).wait_recv()
            across(q, d).start()

    forward(0)
    prow[...] = jnp.zeros_like(prow)
    out_ref[...] = jnp.zeros_like(out_ref)
    for c in swap:
        c.wait_recv()

    def norm(x, y):
        x, y = x.astype(f32), y.astype(f32)
        return jnp.sum(x * x, axis=1, keepdims=True) + jnp.sum(y * y, axis=1, keepdims=True)

    def dot(x, y):
        return lax.dot_general(x, y, NT, preferred_element_type=f32)

    mine = pl.ds(pl.multiple_of(col * half, 16), half)
    own_norm = norm(points[mine, :], other_points[...])
    own_ids = lax.broadcasted_iota(jnp.int32, (half, size), 0) + (me * here + col * half)
    same = lax.broadcasted_iota(jnp.int32, (size, size), 0) == lax.broadcasted_iota(jnp.int32, (size, size), 1)
    eye = jnp.where(same, 1.0, 0.0)

    def panel(q, carry):
        @pl.when(q + 1 < panels)
        def _():
            forward(q + 1)
        for d in range(inner):
            across(q, d).wait_recv()
        span = pl.ds(pl.multiple_of(q * size, size), size)
        ps, po = piv[col, span, :], piv[1 - col, span, :]
        pnorm = norm(ps[:, :fw], po[:, :fw])
        norms[q] = jnp.transpose(jnp.broadcast_to(pnorm, (size, size)))

        def entries(xs, xo, ys, yo, ts, to, n, row_norm):
            cross = dot(xs, ts[:, :fw]) + dot(xo, to[:, :fw])
            schur = dot(ys, ts[:, fw:]) + dot(yo, to[:, fw:])
            return jnp.exp(-(n + row_norm - 2.0 * cross) / feats) + schur / (3.0 * rank)

        def earlier(k, carry):
            other = pl.ds(pl.multiple_of(k * size, size), size)
            ts, to = piv[col, other, :], piv[1 - col, other, :]
            row_norm = norms[k][0:1, :]
            m = entries(ps[:, :fw], po[:, :fw], ps[:, fw:], po[:, fw:], ts, to, pnorm, row_norm)
            m = m - dot(prow[q], prow[k])
            prow[q, :, other] = lax.dot_general(m, inv[k], NT, precision=HIGH,
                                                preferred_element_type=f32).astype(bf16)
            return carry

        lax.fori_loop(0, q, earlier, 0)
        row_norm = norms[q][0:1, :]
        a[...] = (entries(ps[:, :fw], po[:, :fw], ps[:, fw:], po[:, fw:], ps, po, pnorm, row_norm)
                  + RIDGE_LEVEL * eye - dot(prow[q], prow[q]))
        e = inv.at[q]
        e[...] = eye
        ids = owners[pl.ds(q, 1), :] * here + slots[pl.ds(q, 1), :]
        columns = (entries(points[mine, :], other_points[...], factor[mine, :], other_factor[...], ps, po,
                           own_norm, row_norm)
                   + jnp.where(own_ids == ids, RIDGE_LEVEL, 0.0) - dot(out_ref[...], prow[q]))
        factor_block(size, a, e, rows, None, wide)
        out_ref[:, span] = lax.dot_general(columns, e[...], NT, precision=HIGH,
                                           preferred_element_type=f32).astype(bf16)
        return carry

    lax.fori_loop(0, panels, panel, 0)
    for c in step_a + swap:
        c.wait_send()
    for q in range(panels):
        @pl.when(layer != q)
        def _():
            to_owner(q).wait_send()

        @pl.when(layer == q)
        def _():
            for d in range(1, outer):
                spread(q, (q + d) % outer).wait_send()
        for d in range(1, inner):
            around(q, d).wait_send()
        for d in range(inner):
            across(q, d).wait_send()


def gram_kernel(inner, outer, scale, built, factor, weights, own_cols, gram,
                theirs, part, keep, buf_a, mid, acc, buf_b,
                a_send, a_recv, b_send, b_recv, x_send, x_recv):
    me = lax.axis_index("rows")
    col = lax.axis_index("cols")
    place, layer = me % inner, me // inner
    half, wide = built.shape
    width = own_cols.shape[1]
    rank = factor.shape[1]
    chunk = gram.shape[0]
    f32 = jnp.float32
    greet(me, col, inner, outer)
    swap = remote(built, theirs, x_send, x_recv, me, 1 - col)
    swap.start()
    lanes = pl.ds(pl.multiple_of(col * width, 128), width)

    def add(source, which, start):
        span = pl.ds(pl.multiple_of(which * half, 16), half)
        weighted = (source[...].astype(f32) * weights[span, :]).astype(jnp.bfloat16)
        own = source[:, lanes]
        own_cols[span, :] = own
        old = lax.dot_general(weighted, factor[span, :], TN, preferred_element_type=f32)
        new = lax.dot_general(weighted, own, TN, preferred_element_type=f32)
        if start:
            keep[:, :rank] = old
            keep[:, rank:] = new
        else:
            keep[:, :rank] = (keep[:, :rank] + old) * scale
            keep[:, rank:] = (keep[:, rank:] + new) * scale

    add(built, col, True)
    swap.wait_recv()
    add(theirs, 1 - col, False)
    for z in range(outer):
        for p in range(inner):
            first = (z * inner + p) * chunk
            part[z, p] = keep[first:first + chunk, :].astype(jnp.bfloat16)
    stage = []
    for d in range(1, inner):
        p = (place + d) % inner
        c = remote(part.at[:, p], buf_a.at[d - 1], a_send.at[d - 1], a_recv.at[d - 1], layer * inner + p, col)
        c.start()
        stage.append(c)
    for z in range(outer):
        acc[z] = keep[pl.ds(pl.multiple_of((z * inner + place) * chunk, 8), chunk), :]
    for d in range(1, inner):
        stage[d - 1].wait_recv()
        acc[...] = acc[...] + buf_a[d - 1].astype(f32)
    mid[...] = acc[...].astype(jnp.bfloat16)
    second = []
    for d in range(1, outer):
        z = (layer + d) % outer
        c = remote(mid.at[z], buf_b.at[d - 1], b_send.at[d - 1], b_recv.at[d - 1], z * inner + place, col)
        c.start()
        second.append(c)
    total = acc[layer]
    for d in range(1, outer):
        second[d - 1].wait_recv()
        total = total + buf_b[d - 1].astype(f32)
    gram[...] = total
    for c in stage + second + [swap]:
        c.wait_send()


def body(points, factor, weights, pivot_slots, pivot_owners):
    here, fw = points.shape
    rank = factor.shape[1]
    panels, size = pivot_slots.shape
    rows = lax.axis_size("rows")
    inner = inner_size(rows)
    outer = rows // inner
    count = panels * size
    chunk = count // rows
    width = fw + rank
    half = here // 2
    bf16, f32 = jnp.bfloat16, jnp.float32
    vm = pl.BlockSpec(memory_space=VMEM)
    sem = lambda *n: pltpu.SemaphoreType.DMA(n)
    limit = 60 * 1024 * 1024

    split = 4 if rows % 16 == 0 else inner
    layers = rows // split
    piece = size // split
    built = pl.pallas_call(
        functools.partial(panel_kernel, split, layers),
        out_shape=jax.ShapeDtypeStruct((half, count), bf16),
        in_specs=[vm] * 4, out_specs=vm, name="panels",
        scratch_shapes=[
            VMEM((count, width), bf16), VMEM((2, count, width), bf16),
            VMEM((half, fw), bf16), VMEM((half, rank), bf16),
            VMEM((panels, split - 1, piece, width), bf16),
            VMEM((layers, piece, width), bf16),
            VMEM((panels, piece, width), bf16),
            VMEM((panels, size, count), bf16),
            VMEM((panels, size, size), f32), VMEM((panels, size, size), f32), VMEM((size, size), f32),
            VMEM((BLOCK, size), f32), VMEM((BLOCK, BLOCK, size), f32),
            sem(panels, split - 1), sem(panels, split - 1), sem(panels), sem(layers),
            sem(layers), sem(panels), sem(panels, split - 1), sem(panels, split - 1),
            sem(panels, split), sem(panels, split), sem(2), sem(2),
        ],
        compiler_params=pltpu.CompilerParams(collective_id=0, has_side_effects=True, vmem_limit_bytes=limit),
    )(pivot_slots, pivot_owners, points, factor)

    scale = size / math.sqrt(here * rows)
    gw = rank + count // 2
    own_cols, gram = pl.pallas_call(
        functools.partial(gram_kernel, inner, outer, scale),
        out_shape=(
            jax.ShapeDtypeStruct((here, count // 2), bf16),
            jax.ShapeDtypeStruct((chunk, gw), f32),
        ),
        in_specs=[vm] * 3, out_specs=(vm,) * 2, name="gram",
        scratch_shapes=[
            VMEM((half, count), bf16),
            VMEM((outer, inner, chunk, gw), bf16),
            VMEM((count, gw), f32),
            VMEM((inner - 1, outer, chunk, gw), bf16),
            VMEM((outer, chunk, gw), bf16),
            VMEM((outer, chunk, gw), f32),
            VMEM((outer - 1, chunk, gw), bf16),
            sem(inner - 1), sem(inner - 1), sem(outer - 1), sem(outer - 1),
            pltpu.SemaphoreType.DMA, pltpu.SemaphoreType.DMA,
        ],
        compiler_params=pltpu.CompilerParams(collective_id=1, has_side_effects=True, vmem_limit_bytes=limit),
    )(built, factor, weights[:, None])
    return own_cols, gram[:, :rank], gram[:, rank:]


def solution(mesh):
    return jax.shard_map(
        body,
        mesh=mesh,
        in_specs=(P("rows", "cols"), P("rows", "cols"), P("rows"), P(), P()),
        out_specs=(P("rows", "cols"), P("rows", "cols"), P("rows", "cols")),
        check_vma=False,
    )
```

```python
import functools
import math

import jax
import jax.numpy as jnp
from jax import lax
from jax.experimental import pallas as pl
from jax.experimental.pallas import tpu as pltpu
from jax.sharding import PartitionSpec as P

RIDGE_LEVEL = 1.0
BLOCK = 8
VMEM = pltpu.VMEM
HIGH = lax.Precision.HIGHEST
NT = (((1,), (1,)), ((), ()))
TN = (((0,), (0,)), ((), ()))


def inner_size(rows):
    inner = 1
    while inner * inner * 4 <= rows:
        inner *= 2
    return inner


def remote(src, dst, send, recv, row, col):
    return pltpu.make_async_remote_copy(
        src_ref=src, dst_ref=dst, send_sem=send, recv_sem=recv,
        device_id=(row, col), device_id_type=pl.DeviceIdType.MESH,
    )


def greet(me, col, inner, outer):
    place, layer = me % inner, me // inner
    barrier = pltpu.get_barrier_semaphore()
    peers = [(me, 1 - col)]
    peers += [(layer * inner + (place + d) % inner, col) for d in range(1, inner)]
    peers += [(((layer + d) % outer) * inner + place, col) for d in range(1, outer)]
    for peer in peers:
        pl.semaphore_signal(barrier, inc=1, device_id=peer, device_id_type=pl.DeviceIdType.MESH)
    pl.semaphore_wait(barrier, len(peers))


def factor_block(size, a, e, rows, outs, wide):
    for first in range(0, size, BLOCK):
        span = slice(first, first + BLOCK)
        strip = a[span, :]
        for k in range(BLOCK):
            wide[k] = jnp.broadcast_to(strip[:, first + k:first + k + 1], (BLOCK, size))
        d = {(i, k): wide[k, i:i + 1, :] for i in range(BLOCK) for k in range(i + 1)}
        r = [a[first + i:first + i + 1, :] for i in range(BLOCK)]
        s = [e[first + i:first + i + 1, :] for i in range(BLOCK)]
        for k in range(BLOCK):
            scale = lax.rsqrt(d[k, k])
            r[k] = r[k] * scale
            s[k] = s[k] * scale
            for i in range(k + 1, BLOCK):
                d[i, k] = d[i, k] * scale
            for i in range(k + 1, BLOCK):
                r[i] = r[i] - d[i, k] * r[k]
                s[i] = s[i] - d[i, k] * s[k]
                for m in range(k + 1, i + 1):
                    d[i, m] = d[i, m] - d[i, k] * d[m, k]
        for k in range(BLOCK):
            rows[k:k + 1, :] = r[k]
            e[first + k:first + k + 1, :] = s[k]
        after = first + BLOCK
        if after < size:
            upper = jnp.transpose(rows[...])
            rest_a = a[after:, :]
            rest_e = e[after:, :]
            for k in range(BLOCK):
                column = upper[after:, k:k + 1]
                rest_a = rest_a - column * rows[k:k + 1, :]
                rest_e = rest_e - column * e[first + k:first + k + 1, :]
            a[after:, :] = rest_a
            e[after:, :] = rest_e


def panel_kernel(inner, outer, slots, owners, points, factor, out_ref, other_ref,
                 part, piv, other_points, other_factor, buf_a, buf_b, acc,
                 prow, inv, norms, a, rows, wide,
                 a_send, a_recv, b_send, b_recv, f_send, f_recv,
                 d_send, d_recv, e_send, e_recv, x_send, x_recv):
    me = lax.axis_index("rows")
    col = lax.axis_index("cols")
    place, layer = me % inner, me // inner
    panels, size = slots.shape
    here, fw = points.shape
    half = here // 2
    feats, rank = 2 * fw, 2 * factor.shape[1]
    chunk = size // inner
    f32, bf16 = jnp.float32, jnp.bfloat16
    greet(me, col, inner, outer)

    def piece(q, p):
        return pl.ds(pl.multiple_of(q * size + p * chunk, chunk), chunk)

    def turned(row):
        return jnp.transpose(jnp.broadcast_to(row, (size, size)))

    spots = lax.broadcasted_iota(jnp.int32, (size, here), 1) + me * here
    step_a = []
    for q in range(panels):
        ids = (owners[q:q + 1, :] * here + slots[q:q + 1, :]).astype(f32)
        hot = jnp.where(spots == turned(ids)[:, 0:1].astype(jnp.int32), 1.0, 0.0).astype(bf16)
        span = slice(q * size, (q + 1) * size)
        part[span, :fw] = jnp.dot(hot, points[...], preferred_element_type=f32).astype(bf16)
        part[span, fw:] = jnp.dot(hot, factor[...], preferred_element_type=f32).astype(bf16)
        for d in range(1, inner):
            p = (place + d) % inner
            c = remote(part.at[piece(q, p)], buf_a.at[q, d - 1], a_send.at[q, d - 1], a_recv.at[q, d - 1],
                       layer * inner + p, col)
            c.start()
            step_a.append(c)
    theirs = pl.ds(pl.multiple_of((1 - col) * half, 16), half)
    swap = [
        remote(points.at[theirs], other_points, x_send.at[0], x_recv.at[0], me, 1 - col),
        remote(factor.at[theirs], other_factor, x_send.at[1], x_recv.at[1], me, 1 - col),
    ]
    for c in swap:
        c.start()

    def along(q, d):
        return remote(acc.at[q], buf_b.at[q, d - 1], b_send.at[q, d - 1], b_recv.at[q, d - 1],
                      ((layer + d) % outer) * inner + place, col)

    def around(q, d):
        it = piv.at[col, piece(q, place)]
        return remote(it, it, d_send.at[q, d - 1], d_recv.at[q, d - 1], layer * inner + (place + d) % inner, col)

    def across(q, d):
        it = piv.at[col, piece(q, (place + inner - d) % inner)]
        return remote(it, it, e_send.at[q, d], e_recv.at[q, d], me, 1 - col)

    def swap_panel(q):
        span = pl.ds(pl.multiple_of(q * size, size), size)
        return remote(out_ref.at[:, span], other_ref.at[:, span], f_send.at[q], f_recv.at[q], me, 1 - col)

    def layer_sum(q):
        total = part[piece(q, place), :]
        for d in range(1, inner):
            step_a[q * (inner - 1) + d - 1].wait_recv()
            total = total + buf_a[q, d - 1]
        acc[q] = total
        for d in range(1, outer):
            along(q, d).start()

    def whole_sum(q):
        total = acc[q]
        for d in range(1, outer):
            along(q, d).wait_recv()
            total = total + buf_b[q, d - 1]
        piv[col, piece(q, place)] = total
        for d in range(1, inner):
            around(q, d).start()
        across(q, 0).start()

    def forward(q):
        for d in range(1, inner):
            around(q, d).wait_recv()
            across(q, d).start()

    for q in range(panels):
        layer_sum(q)
        if q == min(2, panels - 1):
            whole_sum(0)
    for q in range(1, min(2, panels)):
        whole_sum(q)
    forward(0)
    prow[...] = jnp.zeros_like(prow)
    out_ref[...] = jnp.zeros_like(out_ref)
    for c in swap:
        c.wait_recv()

    def norm(x, y):
        x, y = x.astype(f32), y.astype(f32)
        return jnp.sum(x * x, axis=1, keepdims=True) + jnp.sum(y * y, axis=1, keepdims=True)

    def dot(x, y):
        return lax.dot_general(x, y, NT, preferred_element_type=f32)

    mine = pl.ds(pl.multiple_of(col * half, 16), half)
    own_norm = norm(points[mine, :], other_points[...])
    own_ids = lax.broadcasted_iota(jnp.int32, (half, size), 0) + (me * here + col * half)
    same = lax.broadcasted_iota(jnp.int32, (size, size), 0) == lax.broadcasted_iota(jnp.int32, (size, size), 1)
    eye = jnp.where(same, 1.0, 0.0)

    def panel(q, carry):
        for d in range(inner):
            across(q, d).wait_recv()
        span = pl.ds(pl.multiple_of(q * size, size), size)
        ps, po = piv[col, span, :], piv[1 - col, span, :]
        pnorm = norm(ps[:, :fw], po[:, :fw])
        norms[q] = jnp.transpose(jnp.broadcast_to(pnorm, (size, size)))

        def entries(xs, xo, ys, yo, ts, to, n, row_norm):
            cross = dot(xs, ts[:, :fw]) + dot(xo, to[:, :fw])
            schur = dot(ys, ts[:, fw:]) + dot(yo, to[:, fw:])
            return jnp.exp(-(n + row_norm - 2.0 * cross) / feats) + schur / (3.0 * rank)

        def earlier(k, carry):
            other = pl.ds(pl.multiple_of(k * size, size), size)
            ts, to = piv[col, other, :], piv[1 - col, other, :]
            row_norm = norms[k][0:1, :]
            m = entries(ps[:, :fw], po[:, :fw], ps[:, fw:], po[:, fw:], ts, to, pnorm, row_norm)
            m = m - dot(prow[q], prow[k])
            prow[q, :, other] = lax.dot_general(m, inv[k], NT, precision=HIGH,
                                                preferred_element_type=f32).astype(bf16)
            return carry

        lax.fori_loop(0, q, earlier, 0)
        row_norm = norms[q][0:1, :]
        a[...] = (entries(ps[:, :fw], po[:, :fw], ps[:, fw:], po[:, fw:], ps, po, pnorm, row_norm)
                  + RIDGE_LEVEL * eye - dot(prow[q], prow[q]))
        e = inv.at[q]
        e[...] = eye

        @pl.when(q + 2 < panels)
        def _():
            whole_sum(q + 2)

        @pl.when(q + 1 < panels)
        def _():
            forward(q + 1)
        ids = owners[pl.ds(q, 1), :] * here + slots[pl.ds(q, 1), :]
        columns = (entries(points[mine, :], other_points[...], factor[mine, :], other_factor[...], ps, po,
                           own_norm, row_norm)
                   + jnp.where(own_ids == ids, RIDGE_LEVEL, 0.0) - dot(out_ref[...], prow[q]))
        factor_block(size, a, e, rows, None, wide)
        out_ref[:, span] = lax.dot_general(columns, e[...], NT, precision=HIGH,
                                           preferred_element_type=f32).astype(bf16)
        swap_panel(q).start()
        return carry

    lax.fori_loop(0, panels, panel, 0)
    for c in step_a + swap:
        c.wait_send()
    for q in range(panels):
        swap_panel(q).wait()
        for d in range(1, outer):
            along(q, d).wait_send()
        for d in range(1, inner):
            around(q, d).wait_send()
        for d in range(inner):
            across(q, d).wait_send()


def gram_kernel(inner, outer, scale, built, theirs, factor, weights, own_cols, gram_old, gram_new,
                turned, part, acc, mid, buf_a, buf_b, a_send, a_recv, b_send, b_recv):
    me = lax.axis_index("rows")
    col = lax.axis_index("cols")
    place, layer = me % inner, me // inner
    half, count = built.shape
    width = own_cols.shape[1]
    rank = factor.shape[1]
    chunk = gram_old.shape[0]
    pieces = acc.shape[0]
    wide = acc.shape[3]
    size = weights.shape[1]
    f32, bf16 = jnp.float32, jnp.bfloat16
    greet(me, col, inner, outer)
    lanes = pl.ds(pl.multiple_of(col * width, 128), width)
    for source, which in ((built, col), (theirs, 1 - col)):
        span = pl.ds(pl.multiple_of(which * half, 16), half)
        own_cols[span, :] = source[:, lanes]
        for i in range(half // size):
            row = weights[pl.ds(which * (half // size) + i, 1), :]
            level = jnp.transpose(jnp.broadcast_to(row, (size, size)))[:, 0:1]
            block = source[i * size:(i + 1) * size, :].astype(f32) * level
            first = pl.multiple_of(which * half + i * size, size)
            turned[:, pl.ds(first, size)] = jnp.transpose(block).astype(bf16)

    def step_a(j, d):
        p = (place + d) % inner
        return remote(part.at[j, :, p], buf_a.at[j, d - 1], a_send.at[j, d - 1], a_recv.at[j, d - 1],
                      layer * inner + p, col)

    def step_b(j, d):
        z = (layer + d) % outer
        return remote(mid.at[j, z], buf_b.at[j, d - 1], b_send.at[j, d - 1], b_recv.at[j, d - 1],
                      z * inner + place, col)

    kept = []
    for j in range(pieces):
        if j * wide < rank:
            right = factor[:, j * wide:(j + 1) * wide]
        else:
            right = own_cols[:, j * wide - rank:(j + 1) * wide - rank]
        block = jnp.dot(turned[...], right, preferred_element_type=f32) * scale
        part[j] = block.reshape(outer, inner, chunk, wide).astype(bf16)
        for d in range(1, inner):
            step_a(j, d).start()
    for j in range(pieces):
        total = part[j, :, place].astype(f32)
        for d in range(1, inner):
            step_a(j, d).wait_recv()
            total = total + buf_a[j, d - 1].astype(f32)
        acc[j] = total
        mid[j] = total.astype(bf16)
        for d in range(1, outer):
            step_b(j, d).start()
    for j in range(pieces):
        total = acc[j, layer]
        for d in range(1, outer):
            step_b(j, d).wait_recv()
            total = total + buf_b[j, d - 1].astype(f32)
        if j * wide < rank:
            gram_old[:, j * wide:(j + 1) * wide] = total
        else:
            gram_new[:, j * wide - rank:(j + 1) * wide - rank] = total
    for j in range(pieces):
        for d in range(1, inner):
            step_a(j, d).wait_send()
        for d in range(1, outer):
            step_b(j, d).wait_send()


def body(points, factor, weights, pivot_slots, pivot_owners):
    here, fw = points.shape
    rank = factor.shape[1]
    panels, size = pivot_slots.shape
    rows = lax.axis_size("rows")
    inner = inner_size(rows)
    outer = rows // inner
    count = panels * size
    chunk = count // rows
    width = fw + rank
    half = here // 2
    bf16, f32 = jnp.bfloat16, jnp.float32
    vm = pl.BlockSpec(memory_space=VMEM)
    sem = lambda *n: pltpu.SemaphoreType.DMA(n)
    limit = 60 * 1024 * 1024

    split = 4 if rows % 16 == 0 else inner
    layers = rows // split
    piece = size // split
    built, built_other = pl.pallas_call(
        functools.partial(panel_kernel, split, layers),
        out_shape=(jax.ShapeDtypeStruct((half, count), bf16),) * 2,
        in_specs=[vm] * 4, out_specs=(vm,) * 2, name="panels",
        scratch_shapes=[
            VMEM((count, width), bf16), VMEM((2, count, width), bf16),
            VMEM((half, fw), bf16), VMEM((half, rank), bf16),
            VMEM((panels, split - 1, piece, width), bf16),
            VMEM((panels, layers - 1, piece, width), bf16),
            VMEM((panels, piece, width), bf16),
            VMEM((panels, size, count), bf16),
            VMEM((panels, size, size), f32), VMEM((panels, size, size), f32), VMEM((size, size), f32),
            VMEM((BLOCK, size), f32), VMEM((BLOCK, BLOCK, size), f32),
            sem(panels, split - 1), sem(panels, split - 1), sem(panels, layers - 1), sem(panels, layers - 1),
            sem(panels), sem(panels), sem(panels, split - 1), sem(panels, split - 1),
            sem(panels, split), sem(panels, split), sem(2), sem(2),
        ],
        compiler_params=pltpu.CompilerParams(collective_id=0, has_side_effects=True, vmem_limit_bytes=limit),
    )(pivot_slots, pivot_owners, points, factor)

    scale = size / math.sqrt(here * rows)
    wide = math.gcd(rank, count // 2)
    pieces = (rank + count // 2) // wide
    return pl.pallas_call(
        functools.partial(gram_kernel, inner, outer, scale),
        out_shape=(
            jax.ShapeDtypeStruct((here, count // 2), bf16),
            jax.ShapeDtypeStruct((chunk, rank), f32),
            jax.ShapeDtypeStruct((chunk, count // 2), f32),
        ),
        in_specs=[vm] * 4, out_specs=(vm,) * 3, name="gram",
        scratch_shapes=[
            VMEM((count, here), bf16),
            VMEM((pieces, outer, inner, chunk, wide), bf16),
            VMEM((pieces, outer, chunk, wide), f32),
            VMEM((pieces, outer, chunk, wide), bf16),
            VMEM((pieces, inner - 1, outer, chunk, wide), bf16),
            VMEM((pieces, outer - 1, chunk, wide), bf16),
            sem(pieces, inner - 1), sem(pieces, inner - 1), sem(pieces, outer - 1), sem(pieces, outer - 1),
        ],
        compiler_params=pltpu.CompilerParams(collective_id=1, has_side_effects=True, vmem_limit_bytes=limit),
    )(built, built_other, factor, weights.reshape(here // size, size))


def solution(mesh):
    return jax.shard_map(
        body,
        mesh=mesh,
        in_specs=(P("rows", "cols"), P("rows", "cols"), P("rows"), P(), P()),
        out_specs=(P("rows", "cols"), P("rows", "cols"), P("rows", "cols")),
        check_vma=False,
    )
```

```python
import functools
import math

import jax
import jax.numpy as jnp
from jax import lax
from jax.experimental import pallas as pl
from jax.experimental.pallas import tpu as pltpu
from jax.sharding import PartitionSpec as P

RIDGE_LEVEL = 1.0
BLOCK = 8
VMEM = pltpu.VMEM
HIGH = lax.Precision.HIGHEST
NT = (((1,), (1,)), ((), ()))
TN = (((0,), (0,)), ((), ()))


def remote(src, dst, send, recv, row, col):
    return pltpu.make_async_remote_copy(
        src_ref=src, dst_ref=dst, send_sem=send, recv_sem=recv,
        device_id=(row, col), device_id_type=pl.DeviceIdType.MESH,
    )


def greet(me, col, inner, outer):
    place, layer = me % inner, me // inner
    barrier = pltpu.get_barrier_semaphore()
    peers = [(me, 1 - col)]
    peers += [(layer * inner + (place + d) % inner, col) for d in range(1, inner)]
    peers += [(((layer + d) % outer) * inner + place, col) for d in range(1, outer)]
    for peer in peers:
        pl.semaphore_signal(barrier, inc=1, device_id=peer, device_id_type=pl.DeviceIdType.MESH)
    pl.semaphore_wait(barrier, len(peers))


def factor_block(size, a, e, rows, outs, wide):
    for first in range(0, size, BLOCK):
        span = slice(first, first + BLOCK)
        strip = a[span, :]
        for k in range(BLOCK):
            wide[k] = jnp.broadcast_to(strip[:, first + k:first + k + 1], (BLOCK, size))
        d = {(i, k): wide[k, i:i + 1, :] for i in range(BLOCK) for k in range(i + 1)}
        r = [a[first + i:first + i + 1, :] for i in range(BLOCK)]
        s = [e[first + i:first + i + 1, :] for i in range(BLOCK)]
        for k in range(BLOCK):
            scale = lax.rsqrt(d[k, k])
            r[k] = r[k] * scale
            s[k] = s[k] * scale
            for i in range(k + 1, BLOCK):
                d[i, k] = d[i, k] * scale
            for i in range(k + 1, BLOCK):
                r[i] = r[i] - d[i, k] * r[k]
                s[i] = s[i] - d[i, k] * s[k]
                for m in range(k + 1, i + 1):
                    d[i, m] = d[i, m] - d[i, k] * d[m, k]
        for k in range(BLOCK):
            rows[k:k + 1, :] = r[k]
            e[first + k:first + k + 1, :] = s[k]
        after = first + BLOCK
        if after < size:
            upper = jnp.transpose(rows[...])
            rest_a = a[after:, :]
            rest_e = e[after:, :]
            for k in range(BLOCK):
                column = upper[after:, k:k + 1]
                rest_a = rest_a - column * rows[k:k + 1, :]
                rest_e = rest_e - column * e[first + k:first + k + 1, :]
            a[after:, :] = rest_a
            e[after:, :] = rest_e


def panel_kernel(inner, outer, scale_by, slots, owners, points, factor, weights, own_cols, gram_old, gram_new,
                 out_ref, other_ref, level_t, gp, ga, gacc, gmid, gb, nw, na, nacc, nmid, nb,
                 ga_send, ga_recv, gb_send, gb_recv, na_send, na_recv, nb_send, nb_recv,
                 part, piv, other_points, other_factor, buf_a, buf_b, acc,
                 prow, inv, norms, a, rows, wide,
                 a_send, a_recv, b_send, b_recv, f_send, f_recv,
                 d_send, d_recv, e_send, e_recv, x_send, x_recv):
    me = lax.axis_index("rows")
    col = lax.axis_index("cols")
    place, layer = me % inner, me // inner
    panels, size = slots.shape
    here, fw = points.shape
    half = here // 2
    feats, rank = 2 * fw, 2 * factor.shape[1]
    chunk = size // inner
    f32, bf16 = jnp.float32, jnp.bfloat16
    greet(me, col, inner, outer)

    def piece(q, p):
        return pl.ds(pl.multiple_of(q * size + p * chunk, chunk), chunk)

    def turned(row):
        return jnp.transpose(jnp.broadcast_to(row, (size, size)))

    spots = lax.broadcasted_iota(jnp.int32, (size, here), 1) + me * here
    step_a = []
    for q in range(panels):
        ids = (owners[q:q + 1, :] * here + slots[q:q + 1, :]).astype(f32)
        hot = jnp.where(spots == turned(ids)[:, 0:1].astype(jnp.int32), 1.0, 0.0).astype(bf16)
        span = slice(q * size, (q + 1) * size)
        part[span, :fw] = jnp.dot(hot, points[...], preferred_element_type=f32).astype(bf16)
        part[span, fw:] = jnp.dot(hot, factor[...], preferred_element_type=f32).astype(bf16)
        for d in range(1, inner):
            p = (place + d) % inner
            c = remote(part.at[piece(q, p)], buf_a.at[q, d - 1], a_send.at[q, d - 1], a_recv.at[q, d - 1],
                       layer * inner + p, col)
            c.start()
            step_a.append(c)
    theirs = pl.ds(pl.multiple_of((1 - col) * half, 16), half)
    swap = [
        remote(points.at[theirs], other_points, x_send.at[0], x_recv.at[0], me, 1 - col),
        remote(factor.at[theirs], other_factor, x_send.at[1], x_recv.at[1], me, 1 - col),
    ]
    for c in swap:
        c.start()

    def along(q, d):
        return remote(acc.at[q], buf_b.at[q, d - 1], b_send.at[q, d - 1], b_recv.at[q, d - 1],
                      ((layer + d) % outer) * inner + place, col)

    def around(q, d):
        it = piv.at[col, piece(q, place)]
        return remote(it, it, d_send.at[q, d - 1], d_recv.at[q, d - 1], layer * inner + (place + d) % inner, col)

    def across(q, d):
        it = piv.at[col, piece(q, (place + inner - d) % inner)]
        return remote(it, it, e_send.at[q, d], e_recv.at[q, d], me, 1 - col)

    def swap_panel(q):
        span = pl.ds(pl.multiple_of(q * size, size), size)
        return remote(out_ref.at[:, span], other_ref.at[:, span], f_send.at[q], f_recv.at[q], me, 1 - col)

    def layer_sum(q):
        total = part[piece(q, place), :]
        for d in range(1, inner):
            step_a[q * (inner - 1) + d - 1].wait_recv()
            total = total + buf_a[q, d - 1]
        acc[q] = total
        for d in range(1, outer):
            along(q, d).start()

    def whole_sum(q):
        total = acc[q]
        for d in range(1, outer):
            along(q, d).wait_recv()
            total = total + buf_b[q, d - 1]
        piv[col, piece(q, place)] = total
        for d in range(1, inner):
            around(q, d).start()
        across(q, 0).start()

    def forward(q):
        for d in range(1, inner):
            around(q, d).wait_recv()
            across(q, d).start()

    for q in range(panels):
        layer_sum(q)
        if q == min(2, panels - 1):
            whole_sum(0)
    forward(0)
    for q in range(1, min(2, panels)):
        whole_sum(q)
    prow[...] = jnp.zeros_like(prow)
    out_ref[...] = jnp.zeros_like(out_ref)
    for c in swap:
        c.wait_recv()

    def norm(x, y):
        x, y = x.astype(f32), y.astype(f32)
        return jnp.sum(x * x, axis=1, keepdims=True) + jnp.sum(y * y, axis=1, keepdims=True)

    def dot(x, y):
        return lax.dot_general(x, y, NT, preferred_element_type=f32)

    mine = pl.ds(pl.multiple_of(col * half, 16), half)
    own_norm = norm(points[mine, :], other_points[...])
    own_ids = lax.broadcasted_iota(jnp.int32, (half, size), 0) + (me * here + col * half)
    same = lax.broadcasted_iota(jnp.int32, (size, size), 0) == lax.broadcasted_iota(jnp.int32, (size, size), 1)
    eye = jnp.where(same, 1.0, 0.0)

    runs = gp.shape[1]
    lines = gp.shape[3]
    width = own_cols.shape[1]
    wide_lanes = pl.ds(pl.multiple_of(col * width, 128), width)

    def gram_a(k, d):
        p = (place + d) % inner
        return remote(gp.at[k, :, p], ga.at[k, d - 1], ga_send.at[k, d - 1], ga_recv.at[k, d - 1],
                      layer * inner + p, col)

    def gram_b(k, i):
        target = k * runs + i
        slot = (layer - target + 2 * outer - 1) % outer
        return remote(gmid.at[k, i], gb.at[slot], gb_send.at[k, i], gb_recv.at[slot], target * inner + place, col)

    def gram_got(d):
        return remote(gmid.at[0, 0], gb.at[d - 1], gb_send.at[0, 0], gb_recv.at[d - 1],
                      ((layer + d) % outer) * inner + place, col)

    def new_a(d):
        p = (place + d) % inner
        return remote(nw.at[:, p], na.at[d - 1], na_send.at[d - 1], na_recv.at[d - 1], layer * inner + p, col)

    def new_b(d):
        z = (layer + d) % outer
        return remote(nmid.at[z], nb.at[d - 1], nb_send.at[d - 1], nb_recv.at[d - 1], z * inner + place, col)

    def gram_block(k):
        swap_panel(k).wait_recv()
        lanes = pl.ds(pl.multiple_of(k * size, size), size)
        for source, which in ((out_ref, col), (other_ref, 1 - col)):
            for i in range(half // size):
                level = turned(weights[pl.ds(which * (half // size) + i, 1), :])[:, 0:1]
                block = source[i * size:(i + 1) * size, lanes].astype(f32) * level
                first = pl.multiple_of(which * half + i * size, size)
                level_t[lanes, pl.ds(first, size)] = jnp.transpose(block).astype(bf16)
        block = jnp.dot(level_t[lanes, :], factor[...], preferred_element_type=f32) * scale_by
        gp[k] = block.reshape(runs, inner, lines, factor.shape[1]).astype(bf16)
        for d in range(1, inner):
            gram_a(k, d).start()

    def gram_sum(k):
        total = gp[k, :, place].astype(f32)
        for d in range(1, inner):
            gram_a(k, d).wait_recv()
            total = total + ga[k, d - 1].astype(f32)
        gacc[k] = total
        gmid[k] = total.astype(bf16)
        for i in range(runs):
            @pl.when(layer != k * runs + i)
            def _():
                gram_b(k, i).start()

    def panel(q, carry):
        for d in range(inner):
            across(q, d).wait_recv()
        span = pl.ds(pl.multiple_of(q * size, size), size)
        ps, po = piv[col, span, :], piv[1 - col, span, :]
        pnorm = norm(ps[:, :fw], po[:, :fw])
        norms[q] = jnp.transpose(jnp.broadcast_to(pnorm, (size, size)))

        def entries(xs, xo, ys, yo, ts, to, n, row_norm):
            cross = dot(xs, ts[:, :fw]) + dot(xo, to[:, :fw])
            schur = dot(ys, ts[:, fw:]) + dot(yo, to[:, fw:])
            return jnp.exp(-(n + row_norm - 2.0 * cross) / feats) + schur / (3.0 * rank)

        def earlier(k, carry):
            other = pl.ds(pl.multiple_of(k * size, size), size)
            ts, to = piv[col, other, :], piv[1 - col, other, :]
            row_norm = norms[k][0:1, :]
            m = entries(ps[:, :fw], po[:, :fw], ps[:, fw:], po[:, fw:], ts, to, pnorm, row_norm)
            m = m - dot(prow[q], prow[k])
            prow[q, :, other] = lax.dot_general(m, inv[k], NT, precision=HIGH,
                                                preferred_element_type=f32).astype(bf16)
            return carry

        lax.fori_loop(0, q, earlier, 0)
        row_norm = norms[q][0:1, :]
        a[...] = (entries(ps[:, :fw], po[:, :fw], ps[:, fw:], po[:, fw:], ps, po, pnorm, row_norm)
                  + RIDGE_LEVEL * eye - dot(prow[q], prow[q]))
        e = inv.at[q]
        e[...] = eye

        @pl.when(q + 2 < panels)
        def _():
            whole_sum(q + 2)

        @pl.when(q + 1 < panels)
        def _():
            forward(q + 1)

        @pl.when(q > 1)
        def _():
            gram_sum(q - 2)

        @pl.when(q > 0)
        def _():
            gram_block(q - 1)
        ids = owners[pl.ds(q, 1), :] * here + slots[pl.ds(q, 1), :]
        columns = (entries(points[mine, :], other_points[...], factor[mine, :], other_factor[...], ps, po,
                           own_norm, row_norm)
                   + jnp.where(own_ids == ids, RIDGE_LEVEL, 0.0) - dot(out_ref[...], prow[q]))
        factor_block(size, a, e, rows, None, wide)
        out_ref[:, span] = lax.dot_general(columns, e[...], NT, precision=HIGH,
                                           preferred_element_type=f32).astype(bf16)
        swap_panel(q).start()
        return carry

    lax.fori_loop(0, panels, panel, 0)
    if panels > 1:
        gram_sum(panels - 2)
    gram_block(panels - 1)
    for source, which in ((out_ref, col), (other_ref, 1 - col)):
        own_cols[pl.ds(pl.multiple_of(which * half, 16), half), :] = source[:, wide_lanes]
    block = jnp.dot(level_t[...], own_cols[...], preferred_element_type=f32) * scale_by
    nw[...] = block.reshape(outer, inner, lines, width).astype(bf16)
    for d in range(1, inner):
        new_a(d).start()
    gram_sum(panels - 1)
    total = nw[:, place].astype(f32)
    for d in range(1, inner):
        new_a(d).wait_recv()
        total = total + na[d - 1].astype(f32)
    nacc[...] = total
    nmid[...] = total.astype(bf16)
    for d in range(1, outer):
        new_b(d).start()
    total = gacc[layer // runs, layer % runs]
    for d in range(1, outer):
        gram_got(d).wait_recv()
        total = total + gb[d - 1].astype(f32)
    gram_old[...] = total
    total = nacc[layer]
    for d in range(1, outer):
        new_b(d).wait_recv()
        total = total + nb[d - 1].astype(f32)
    gram_new[...] = total
    for d in range(1, inner):
        new_a(d).wait_send()
    for d in range(1, outer):
        new_b(d).wait_send()
    for c in step_a + swap:
        c.wait_send()
    for q in range(panels):
        swap_panel(q).wait_send()
        for d in range(1, inner):
            gram_a(q, d).wait_send()
        for i in range(runs):
            @pl.when(layer != q * runs + i)
            def _():
                gram_b(q, i).wait_send()
        for d in range(1, outer):
            along(q, d).wait_send()
        for d in range(1, inner):
            around(q, d).wait_send()
        for d in range(inner):
            across(q, d).wait_send()


def body(points, factor, weights, pivot_slots, pivot_owners):
    here, fw = points.shape
    rank = factor.shape[1]
    panels, size = pivot_slots.shape
    rows = lax.axis_size("rows")
    count = panels * size
    chunk = count // rows
    width = fw + rank
    half = here // 2
    bf16, f32 = jnp.bfloat16, jnp.float32
    vm = pl.BlockSpec(memory_space=VMEM)
    sem = lambda *n: pltpu.SemaphoreType.DMA(n)
    limit = 60 * 1024 * 1024

    split = rows // panels if rows < panels * panels else panels
    layers = rows // split
    piece = size // split
    runs = layers // panels
    share = count // 2
    scale = size / math.sqrt(here * rows)
    return pl.pallas_call(
        functools.partial(panel_kernel, split, layers, scale),
        out_shape=(
            jax.ShapeDtypeStruct((here, share), bf16),
            jax.ShapeDtypeStruct((chunk, rank), f32),
            jax.ShapeDtypeStruct((chunk, share), f32),
        ),
        in_specs=[vm] * 5, out_specs=(vm,) * 3, name="panels",
        scratch_shapes=[
            VMEM((half, count), bf16), VMEM((half, count), bf16), VMEM((count, here), bf16),
            VMEM((panels, runs, split, chunk, rank), bf16),
            VMEM((panels, split - 1, runs, chunk, rank), bf16),
            VMEM((panels, runs, chunk, rank), f32), VMEM((panels, runs, chunk, rank), bf16),
            VMEM((layers, chunk, rank), bf16),
            VMEM((layers, split, chunk, share), bf16),
            VMEM((split - 1, layers, chunk, share), bf16),
            VMEM((layers, chunk, share), f32), VMEM((layers, chunk, share), bf16),
            VMEM((layers - 1, chunk, share), bf16),
            sem(panels, split - 1), sem(panels, split - 1), sem(panels, runs), sem(layers),
            sem(split - 1), sem(split - 1), sem(layers - 1), sem(layers - 1),
            VMEM((count, width), bf16), VMEM((2, count, width), bf16),
            VMEM((half, fw), bf16), VMEM((half, rank), bf16),
            VMEM((panels, split - 1, piece, width), bf16),
            VMEM((panels, layers - 1, piece, width), bf16),
            VMEM((panels, piece, width), bf16),
            VMEM((panels, size, count), bf16),
            VMEM((panels, size, size), f32), VMEM((panels, size, size), f32), VMEM((size, size), f32),
            VMEM((BLOCK, size), f32), VMEM((BLOCK, BLOCK, size), f32),
            sem(panels, split - 1), sem(panels, split - 1), sem(panels, layers - 1), sem(panels, layers - 1),
            sem(panels), sem(panels), sem(panels, split - 1), sem(panels, split - 1),
            sem(panels, split), sem(panels, split), sem(2), sem(2),
        ],
        compiler_params=pltpu.CompilerParams(collective_id=0, has_side_effects=True, vmem_limit_bytes=limit),
    )(pivot_slots, pivot_owners, points, factor, weights.reshape(here // size, size))


def solution(mesh):
    return jax.shard_map(
        body,
        mesh=mesh,
        in_specs=(P("rows", "cols"), P("rows", "cols"), P("rows"), P(), P()),
        out_specs=(P("rows", "cols"), P("rows", "cols"), P("rows", "cols")),
        check_vma=False,
    )
```

```python
import functools
import math

import jax
import jax.numpy as jnp
from jax import lax
from jax.experimental import pallas as pl
from jax.experimental.pallas import tpu as pltpu
from jax.sharding import PartitionSpec as P

RIDGE_LEVEL = 1.0
BLOCK = 8
VMEM = pltpu.VMEM
HIGH = lax.Precision.HIGHEST
NT = (((1,), (1,)), ((), ()))
TN = (((0,), (0,)), ((), ()))


def remote(src, dst, send, recv, row, col):
    return pltpu.make_async_remote_copy(
        src_ref=src, dst_ref=dst, send_sem=send, recv_sem=recv,
        device_id=(row, col), device_id_type=pl.DeviceIdType.MESH,
    )


def greet(me, col, inner, outer):
    place, layer = me % inner, me // inner
    barrier = pltpu.get_barrier_semaphore()
    peers = [(me, 1 - col)]
    peers += [(layer * inner + (place + d) % inner, col) for d in range(1, inner)]
    peers += [(((layer + d) % outer) * inner + place, col) for d in range(1, outer)]
    for peer in peers:
        pl.semaphore_signal(barrier, inc=1, device_id=peer, device_id_type=pl.DeviceIdType.MESH)
    pl.semaphore_wait(barrier, len(peers))


def factor_block(size, a, e, rows, outs, wide):
    for first in range(0, size, BLOCK):
        span = slice(first, first + BLOCK)
        strip = a[span, :]
        for k in range(BLOCK):
            wide[first // BLOCK % 2 * BLOCK + k] = jnp.broadcast_to(strip[:, first + k:first + k + 1], (BLOCK, size))
        d = {(i, k): wide[first // BLOCK % 2 * BLOCK + k, i:i + 1, :] for i in range(BLOCK) for k in range(i + 1)}
        r = [a[first + i:first + i + 1, :] for i in range(BLOCK)]
        s = [e[first + i:first + i + 1, :] for i in range(BLOCK)]
        for k in range(BLOCK):
            scale = lax.rsqrt(d[k, k])
            r[k] = r[k] * scale
            s[k] = s[k] * scale
            for i in range(k + 1, BLOCK):
                d[i, k] = d[i, k] * scale
            for i in range(k + 1, BLOCK):
                r[i] = r[i] - d[i, k] * r[k]
                s[i] = s[i] - d[i, k] * s[k]
                for m in range(k + 1, i + 1):
                    d[i, m] = d[i, m] - d[i, k] * d[m, k]
        base = BLOCK * (first // BLOCK % 2)
        for k in range(BLOCK):
            rows[base + k:base + k + 1, :] = r[k]
            e[first + k:first + k + 1, :] = s[k]
        after = first + BLOCK
        if after < size:
            upper = jnp.transpose(rows[base:base + BLOCK, :])
            for low, high in ((after, after + BLOCK), (after + BLOCK, size)):
                if low < high:
                    rest_a = a[low:high, :]
                    rest_e = e[low:high, :]
                    for k in range(BLOCK):
                        column = upper[low:high, k:k + 1]
                        rest_a = rest_a - column * rows[base + k:base + k + 1, :]
                        rest_e = rest_e - column * e[first + k:first + k + 1, :]
                    a[low:high, :] = rest_a
                    e[low:high, :] = rest_e


def panel_kernel(inner, outer, scale_by, slots, owners, points, factor, weights, own_cols, gram_old, gram_new,
                 out_ref, other_ref, level_t, gp, ga, gacc, gmid, gb, nw, na, nacc, nmid, nb,
                 ga_send, ga_recv, gb_send, gb_recv, na_send, na_recv, nb_send, nb_recv,
                 part, piv, other_points, other_factor, buf_a, buf_b, acc,
                 prow, inv, norms, a, rows, wide,
                 a_send, a_recv, b_send, b_recv, f_send, f_recv,
                 d_send, d_recv, e_send, e_recv, x_send, x_recv):
    me = lax.axis_index("rows")
    col = lax.axis_index("cols")
    place, layer = me % inner, me // inner
    panels, size = slots.shape
    here, fw = points.shape
    half = here // 2
    feats, rank = 2 * fw, 2 * factor.shape[1]
    chunk = size // inner
    f32, bf16 = jnp.float32, jnp.bfloat16
    greet(me, col, inner, outer)

    def piece(q, p):
        return pl.ds(pl.multiple_of(q * size + p * chunk, chunk), chunk)

    def turned(row):
        return jnp.transpose(jnp.broadcast_to(row, (size, size)))

    spots = lax.broadcasted_iota(jnp.int32, (size, here), 1) + me * here
    step_a = []
    for q in range(panels):
        ids = (owners[q:q + 1, :] * here + slots[q:q + 1, :]).astype(f32)
        hot = jnp.where(spots == turned(ids)[:, 0:1].astype(jnp.int32), 1.0, 0.0).astype(bf16)
        span = slice(q * size, (q + 1) * size)
        part[span, :fw] = jnp.dot(hot, points[...], preferred_element_type=f32).astype(bf16)
        part[span, fw:] = jnp.dot(hot, factor[...], preferred_element_type=f32).astype(bf16)
        for d in range(1, inner):
            p = (place + d) % inner
            c = remote(part.at[piece(q, p)], buf_a.at[q, d - 1], a_send.at[q, d - 1], a_recv.at[q, d - 1],
                       layer * inner + p, col)
            c.start()
            step_a.append(c)
    theirs = pl.ds(pl.multiple_of((1 - col) * half, 16), half)
    swap = [
        remote(points.at[theirs], other_points, x_send.at[0], x_recv.at[0], me, 1 - col),
        remote(factor.at[theirs], other_factor, x_send.at[1], x_recv.at[1], me, 1 - col),
    ]
    for c in swap:
        c.start()

    def along(q, d):
        return remote(acc.at[q], buf_b.at[q, d - 1], b_send.at[q, d - 1], b_recv.at[q, d - 1],
                      ((layer + d) % outer) * inner + place, col)

    def around(q, d):
        it = piv.at[col, piece(q, place)]
        return remote(it, it, d_send.at[q, d - 1], d_recv.at[q, d - 1], layer * inner + (place + d) % inner, col)

    def across(q, d):
        it = piv.at[col, piece(q, (place + inner - d) % inner)]
        return remote(it, it, e_send.at[q, d], e_recv.at[q, d], me, 1 - col)

    def swap_panel(q):
        span = pl.ds(pl.multiple_of(q * size, size), size)
        return remote(out_ref.at[:, span], other_ref.at[:, span], f_send.at[q], f_recv.at[q], me, 1 - col)

    def layer_sum(q):
        total = part[piece(q, place), :]
        for d in range(1, inner):
            step_a[q * (inner - 1) + d - 1].wait_recv()
            total = total + buf_a[q, d - 1]
        acc[q] = total
        for d in range(1, outer):
            along(q, d).start()

    def whole_sum(q):
        total = acc[q]
        for d in range(1, outer):
            along(q, d).wait_recv()
            total = total + buf_b[q, d - 1]
        piv[col, piece(q, place)] = total
        for d in range(1, inner):
            around(q, d).start()
        across(q, 0).start()

    def forward(q):
        for d in range(1, inner):
            around(q, d).wait_recv()
            across(q, d).start()

    for q in range(panels):
        layer_sum(q)
        if q == min(2, panels - 1):
            whole_sum(0)
    forward(0)
    for q in range(1, min(2, panels)):
        whole_sum(q)
    prow[...] = jnp.zeros_like(prow)
    out_ref[...] = jnp.zeros_like(out_ref)
    for c in swap:
        c.wait_recv()

    def norm(x, y):
        x, y = x.astype(f32), y.astype(f32)
        return jnp.sum(x * x, axis=1, keepdims=True) + jnp.sum(y * y, axis=1, keepdims=True)

    def dot(x, y):
        return lax.dot_general(x, y, NT, preferred_element_type=f32)

    mine = pl.ds(pl.multiple_of(col * half, 16), half)
    own_norm = norm(points[mine, :], other_points[...])
    own_ids = lax.broadcasted_iota(jnp.int32, (half, size), 0) + (me * here + col * half)
    same = lax.broadcasted_iota(jnp.int32, (size, size), 0) == lax.broadcasted_iota(jnp.int32, (size, size), 1)
    eye = jnp.where(same, 1.0, 0.0)

    runs = gp.shape[1]
    lines = gp.shape[3]
    width = own_cols.shape[1]
    wide_lanes = pl.ds(pl.multiple_of(col * width, 128), width)

    def gram_a(k, d):
        p = (place + d) % inner
        return remote(gp.at[k, :, p], ga.at[k, d - 1], ga_send.at[k, d - 1], ga_recv.at[k, d - 1],
                      layer * inner + p, col)

    def gram_b(k, i):
        target = k * runs + i
        slot = (layer - target + 2 * outer - 1) % outer
        return remote(gmid.at[k, i], gb.at[slot], gb_send.at[k, i], gb_recv.at[slot], target * inner + place, col)

    def gram_got(d):
        return remote(gmid.at[0, 0], gb.at[d - 1], gb_send.at[0, 0], gb_recv.at[d - 1],
                      ((layer + d) % outer) * inner + place, col)

    def new_a(d):
        p = (place + d) % inner
        return remote(nw.at[:, p], na.at[d - 1], na_send.at[d - 1], na_recv.at[d - 1], layer * inner + p, col)

    def new_b(d):
        z = (layer + d) % outer
        return remote(nmid.at[z], nb.at[d - 1], nb_send.at[d - 1], nb_recv.at[d - 1], z * inner + place, col)

    def gram_block(k):
        swap_panel(k).wait_recv()
        lanes = pl.ds(pl.multiple_of(k * size, size), size)
        for source, which in ((out_ref, col), (other_ref, 1 - col)):
            for i in range(half // size):
                level = turned(weights[pl.ds(which * (half // size) + i, 1), :])[:, 0:1]
                block = source[i * size:(i + 1) * size, lanes].astype(f32) * level
                first = pl.multiple_of(which * half + i * size, size)
                level_t[lanes, pl.ds(first, size)] = jnp.transpose(block).astype(bf16)
        block = jnp.dot(level_t[lanes, :], factor[...], preferred_element_type=f32) * scale_by
        gp[k] = block.reshape(runs, inner, lines, factor.shape[1]).astype(bf16)
        for d in range(1, inner):
            gram_a(k, d).start()

    def gram_sum(k):
        total = gp[k, :, place].astype(f32)
        for d in range(1, inner):
            gram_a(k, d).wait_recv()
            total = total + ga[k, d - 1].astype(f32)
        gacc[k] = total
        gmid[k] = total.astype(bf16)
        for i in range(runs):
            @pl.when(layer != k * runs + i)
            def _():
                gram_b(k, i).start()

    def panel(q, carry):
        for d in range(inner):
            across(q, d).wait_recv()
        span = pl.ds(pl.multiple_of(q * size, size), size)
        ps, po = piv[col, span, :], piv[1 - col, span, :]
        pnorm = norm(ps[:, :fw], po[:, :fw])
        norms[q] = jnp.transpose(jnp.broadcast_to(pnorm, (size, size)))

        def entries(xs, xo, ys, yo, ts, to, n, row_norm):
            cross = dot(xs, ts[:, :fw]) + dot(xo, to[:, :fw])
            schur = dot(ys, ts[:, fw:]) + dot(yo, to[:, fw:])
            return jnp.exp(-(n + row_norm - 2.0 * cross) / feats) + schur / (3.0 * rank)

        def earlier(k, carry):
            other = pl.ds(pl.multiple_of(k * size, size), size)
            ts, to = piv[col, other, :], piv[1 - col, other, :]
            row_norm = norms[k][0:1, :]
            m = entries(ps[:, :fw], po[:, :fw], ps[:, fw:], po[:, fw:], ts, to, pnorm, row_norm)
            m = m - dot(prow[q], prow[k])
            prow[q, :, other] = lax.dot_general(m, inv[k], NT, precision=HIGH,
                                                preferred_element_type=f32).astype(bf16)
            return carry

        lax.fori_loop(0, q, earlier, 0)
        row_norm = norms[q][0:1, :]
        a[...] = (entries(ps[:, :fw], po[:, :fw], ps[:, fw:], po[:, fw:], ps, po, pnorm, row_norm)
                  + RIDGE_LEVEL * eye - dot(prow[q], prow[q]))
        e = inv.at[q]
        e[...] = eye

        @pl.when(q + 2 < panels)
        def _():
            whole_sum(q + 2)

        @pl.when(q + 1 < panels)
        def _():
            forward(q + 1)

        @pl.when(q > 1)
        def _():
            gram_sum(q - 2)

        @pl.when(q > 0)
        def _():
            gram_block(q - 1)
        ids = owners[pl.ds(q, 1), :] * here + slots[pl.ds(q, 1), :]
        columns = (entries(points[mine, :], other_points[...], factor[mine, :], other_factor[...], ps, po,
                           own_norm, row_norm)
                   + jnp.where(own_ids == ids, RIDGE_LEVEL, 0.0) - dot(out_ref[...], prow[q]))
        factor_block(size, a, e, rows, None, wide)
        out_ref[:, span] = lax.dot_general(columns, e[...], NT, precision=HIGH,
                                           preferred_element_type=f32).astype(bf16)
        swap_panel(q).start()
        return carry

    lax.fori_loop(0, panels, panel, 0)
    if panels > 1:
        gram_sum(panels - 2)
    gram_block(panels - 1)
    for source, which in ((out_ref, col), (other_ref, 1 - col)):
        own_cols[pl.ds(pl.multiple_of(which * half, 16), half), :] = source[:, wide_lanes]
    block = jnp.dot(level_t[...], own_cols[...], preferred_element_type=f32) * scale_by
    nw[...] = block.reshape(outer, inner, lines, width).astype(bf16)
    for d in range(1, inner):
        new_a(d).start()
    gram_sum(panels - 1)
    total = nw[:, place].astype(f32)
    for d in range(1, inner):
        new_a(d).wait_recv()
        total = total + na[d - 1].astype(f32)
    nacc[...] = total
    nmid[...] = total.astype(bf16)
    for d in range(1, outer):
        new_b(d).start()
    total = gacc[layer // runs, layer % runs]
    for d in range(1, outer):
        gram_got(d).wait_recv()
        total = total + gb[d - 1].astype(f32)
    gram_old[...] = total
    total = nacc[layer]
    for d in range(1, outer):
        new_b(d).wait_recv()
        total = total + nb[d - 1].astype(f32)
    gram_new[...] = total
    for d in range(1, inner):
        new_a(d).wait_send()
    for d in range(1, outer):
        new_b(d).wait_send()
    for c in step_a + swap:
        c.wait_send()
    for q in range(panels):
        swap_panel(q).wait_send()
        for d in range(1, inner):
            gram_a(q, d).wait_send()
        for i in range(runs):
            @pl.when(layer != q * runs + i)
            def _():
                gram_b(q, i).wait_send()
        for d in range(1, outer):
            along(q, d).wait_send()
        for d in range(1, inner):
            around(q, d).wait_send()
        for d in range(inner):
            across(q, d).wait_send()


def body(points, factor, weights, pivot_slots, pivot_owners):
    here, fw = points.shape
    rank = factor.shape[1]
    panels, size = pivot_slots.shape
    rows = lax.axis_size("rows")
    count = panels * size
    chunk = count // rows
    width = fw + rank
    half = here // 2
    bf16, f32 = jnp.bfloat16, jnp.float32
    vm = pl.BlockSpec(memory_space=VMEM)
    sem = lambda *n: pltpu.SemaphoreType.DMA(n)
    limit = 60 * 1024 * 1024

    split = rows // panels if rows < panels * panels else panels
    layers = rows // split
    piece = size // split
    runs = layers // panels
    share = count // 2
    scale = size / math.sqrt(here * rows)
    return pl.pallas_call(
        functools.partial(panel_kernel, split, layers, scale),
        out_shape=(
            jax.ShapeDtypeStruct((here, share), bf16),
            jax.ShapeDtypeStruct((chunk, rank), f32),
            jax.ShapeDtypeStruct((chunk, share), f32),
        ),
        in_specs=[vm] * 5, out_specs=(vm,) * 3, name="panels",
        scratch_shapes=[
            VMEM((half, count), bf16), VMEM((half, count), bf16), VMEM((count, here), bf16),
            VMEM((panels, runs, split, chunk, rank), bf16),
            VMEM((panels, split - 1, runs, chunk, rank), bf16),
            VMEM((panels, runs, chunk, rank), f32), VMEM((panels, runs, chunk, rank), bf16),
            VMEM((layers, chunk, rank), bf16),
            VMEM((layers, split, chunk, share), bf16),
            VMEM((split - 1, layers, chunk, share), bf16),
            VMEM((layers, chunk, share), f32), VMEM((layers, chunk, share), bf16),
            VMEM((layers - 1, chunk, share), bf16),
            sem(panels, split - 1), sem(panels, split - 1), sem(panels, runs), sem(layers),
            sem(split - 1), sem(split - 1), sem(layers - 1), sem(layers - 1),
            VMEM((count, width), bf16), VMEM((2, count, width), bf16),
            VMEM((half, fw), bf16), VMEM((half, rank), bf16),
            VMEM((panels, split - 1, piece, width), bf16),
            VMEM((panels, layers - 1, piece, width), bf16),
            VMEM((panels, piece, width), bf16),
            VMEM((panels, size, count), bf16),
            VMEM((panels, size, size), f32), VMEM((panels, size, size), f32), VMEM((size, size), f32),
            VMEM((2 * BLOCK, size), f32), VMEM((2 * BLOCK, BLOCK, size), f32),
            sem(panels, split - 1), sem(panels, split - 1), sem(panels, layers - 1), sem(panels, layers - 1),
            sem(panels), sem(panels), sem(panels, split - 1), sem(panels, split - 1),
            sem(panels, split), sem(panels, split), sem(2), sem(2),
        ],
        compiler_params=pltpu.CompilerParams(collective_id=0, has_side_effects=True, vmem_limit_bytes=limit),
    )(pivot_slots, pivot_owners, points, factor, weights.reshape(here // size, size))


def solution(mesh):
    return jax.shard_map(
        body,
        mesh=mesh,
        in_specs=(P("rows", "cols"), P("rows", "cols"), P("rows"), P(), P()),
        out_specs=(P("rows", "cols"), P("rows", "cols"), P("rows", "cols")),
        check_vma=False,
    )
```
